1024 devices in a mesh: section: 8 (over y), expert: 16 (over z, core), tensor: 8 (over x).
Axes of the slice: x: 8, y: 8, z: 8, core: 2. Of those that a mesh axis runs over, the one named last changes fastest.
Arguments:
- tokens: bfloat16 [8, 16384, 2048], P('section', ('expert', 'tensor')), may hold values from -6 to 6
- routes: int32 [8, 16384, 2], P('section', ('expert', 'tensor')), may hold values from 0 to 15, all different within a row; in each aligned block of 128 rows (0 to 127, 128 to 255, ..., all dimensions but the last counted through in order) at most 32 rows name the same one
- route_weights: float32 [8, 16384, 2], P('section', ('expert', 'tensor')), may hold values from 0.2 to 1
- expert_gate: bfloat16 [8, 16, 2048, 512], P('section', 'expert'), may hold values from -0.125 to 0.125
- expert_up: bfloat16 [8, 16, 2048, 512], P('section', 'expert'), may hold values from -0.125 to 0.125
- expert_down: bfloat16 [8, 16, 512, 2048], P('section', 'expert'), may hold values from -0.25 to 0.25
Outputs:
- layer_out: bfloat16 [8, 16384, 2048], P('section', ('expert', 'tensor'))
- next_input: bfloat16 [8, 16384, 2048], P('section', ('expert', 'tensor'))
The draws below stay inside these ranges and needn't reach their ends.
Inputs may be any that keep to these rules, and one draw needn't show every extreme that they name: Each token names 2 different experts; among the tokens of one device no expert is named by more than 32 routes, a bound that some block reaches.
All inputs are finite; a program needn't handle non-finite values.
Results may differ from the reference program's by a relative error of at most 0.0042.
Values may be sent and summed in bfloat16 or wider, within the bound.
A program may use at most 32 MiB of HBM per device.

```python
import math
import jax
import jax.numpy as jnp
import numpy as np
from jax import lax

D = 2048
FF = 512
TOPK = 2
TOK_DEV = 128
EXPERTS = 16
CAP = 32
TOKENS = 16384
N_SECTION = 8
N_EXPERT = 16
N_TENSOR = 8


def shard_levels(rng, shape, shards, low, high):
    factor_of = 1.0
    for dim, blocks in shards:
        draws = jax.random.uniform(jax.random.fold_in(jax.random.fold_in(rng, 6), dim), (blocks,), jnp.float32, low / len(shards), high / len(shards))
        factor_of = factor_of * jnp.repeat(jnp.exp(draws), shape[dim] // blocks).reshape((-1,) + (1,) * (len(shape) - 1 - dim))
    return factor_of


def routed_block(rng, own, number, rows, amount, top, reach, lean):
    sequence = jax.random.permutation(rng, amount)
    heavy_load, ordinary = portions_of(amount, rows * top, reach, lean, True), portions_of(amount, rows * top, reach, lean, False)
    places = jnp.arange(amount)

    def named(sizes, rotation):
        used = int((sizes > 0).sum())
        fixed = max(1, used // 4)
        shifted = fixed + (places - fixed + rotation * (used - fixed)) % max(1, amount - fixed)
        return jnp.zeros((amount,), jnp.int32).at[sequence[jnp.where(places < fixed, places, shifted)]].set(jnp.asarray(sizes, jnp.int32))

    sizes = jnp.where(number % 4 == 0, named(heavy_load, number // 4), named(ordinary, number - number // 4 - 1))
    mixed = jax.random.permutation(jax.random.fold_in(own, 3), amount)
    source_of, taker = mixed[0:amount // 2 * 2:2], mixed[1:amount // 2 * 2:2]
    room = jnp.minimum(sizes[source_of] - 1, reach - sizes[taker]) // 2
    room = jnp.where((source_of == sequence[0]) | (taker == sequence[0]) | (sizes[taker] == 0), 0, jnp.maximum(room, 0))
    shifted = jax.random.randint(jax.random.fold_in(own, 4), (amount // 2,), 0, 1 << 20) % (room + 1)
    sizes = sizes.at[source_of].add(-shifted).at[taker].add(shifted)
    items = jnp.searchsorted(jnp.cumsum(sizes), jnp.arange(rows * top), side="right").astype(jnp.int32)
    table = items.reshape(top, rows).T
    table = table[jax.random.permutation(jax.random.fold_in(own, 1), rows)]
    rotation = jax.random.randint(jax.random.fold_in(own, 2), (rows, 1), 0, top)
    return jnp.take_along_axis(table, (jnp.arange(top)[None, :] + rotation) % top, axis=1)


def portions_of(count, total, reach, slope, full):
    weights = [(1 << 20) // math.isqrt(standing ** slope) + 1 for standing in range(1, count + 1)]
    largest = reach if full else min(reach, max(-(-total // count), total * weights[0] // sum(weights)))
    least = 1 if total - largest >= count - 1 else 0
    counts, spare = [largest] + [least] * (count - 1), total - largest - least * (count - 1)
    while spare > 0:
        candidates = [i for i in range(1, count) if counts[i] < largest] or [i for i in range(1, count) if counts[i] < reach]
        whole, left = sum([weights[i] for i in candidates]), spare
        for i in candidates:
            addition = min(reach - counts[i], max(1, left * weights[i] // whole), spare)
            counts[i] = counts[i] + addition
            spare = spare - addition
    return np.array(counts)


def noise(rng, dims, scale, limit, shards=(), kind=jnp.bfloat16):
    loudness = shard_levels(rng, dims, shards, -0.22, 0.18) if shards else 1.0
    values = jax.random.normal(rng, dims, jnp.float32) * scale * loudness
    return jnp.minimum(jnp.maximum(values, -limit), limit).astype(kind)


def setup_inputs(seed: int = 0) -> dict:
    key_list = jax.random.split(jax.random.key(seed), 7)
    tokens = noise(key_list[0], (N_SECTION, TOKENS, D), 1.0, 6.0, ((0, 8), (1, 128)))
    routes_keys = jax.random.split(jax.random.fold_in(key_list[1], 1), N_SECTION * TOKENS // TOK_DEV)
    routes_turns = jax.random.permutation(jax.random.fold_in(key_list[1], 3), N_SECTION * TOKENS // TOK_DEV)
    routes = jax.vmap(lambda own, number: routed_block(jax.random.fold_in(key_list[1], 2), own, number, TOK_DEV, EXPERTS, TOPK, CAP, 2))(routes_keys, routes_turns).reshape((N_SECTION, TOKENS, TOPK))
    route_weights = jnp.clip(jnp.exp(math.log(1.0) - 1.609438 * jax.random.uniform(key_list[2], (N_SECTION, TOKENS, TOPK), jnp.float32) ** shard_levels(key_list[2], (N_SECTION, TOKENS, TOPK), ((0, 8), (1, 128)), -0.2, 0.2)), 0.2, 1.0)
    expert_gate = noise(key_list[3], (N_SECTION, EXPERTS, D, FF), D ** -0.5, 0.125, ((0, 8), (1, 16)))
    expert_up = noise(key_list[4], (N_SECTION, EXPERTS, D, FF), D ** -0.5, 0.125, ((0, 8), (1, 16)))
    expert_down = noise(key_list[5], (N_SECTION, EXPERTS, FF, D), FF ** -0.5, 0.25, ((0, 8), (1, 16)))
    return {"tokens": tokens, "routes": routes, "route_weights": route_weights, "expert_gate": expert_gate, "expert_up": expert_up, "expert_down": expert_down}


def one_section(items):
    rows_in, flat_routes, flat_weights, w_gate, w_up, w_down = items
    token_of = (jnp.arange(TOKENS * TOPK, dtype=jnp.int32) // TOPK).astype(jnp.int32)
    slot_total = N_EXPERT * N_TENSOR * CAP

    def per_expert(total, packed):
        expert_id, gate_e, up_e, down_e = packed
        match = flat_routes == expert_id
        picked = jnp.nonzero(match, size=slot_total, fill_value=0)[0].astype(jnp.int32)
        live = jnp.arange(slot_total, dtype=jnp.int32) < jnp.sum(match.astype(jnp.int32))
        source = rows_in[token_of[picked]]
        gate_val = jnp.dot(source, gate_e, preferred_element_type=jnp.float32)
        up_val = jnp.dot(source, up_e, preferred_element_type=jnp.float32)
        hidden = (jax.nn.silu(gate_val) * up_val).astype(jnp.bfloat16)
        result = jnp.dot(hidden, down_e, preferred_element_type=jnp.float32).astype(jnp.bfloat16)
        scaled = jnp.where(live, flat_weights[picked], jnp.zeros_like(flat_weights[picked]))
        total = total.at[token_of[picked]].add(result.astype(jnp.float32) * scaled[:, None])
        return total, None

    start = jnp.zeros((TOKENS, D), jnp.float32)
    routed, _ = lax.scan(per_expert, start, (jnp.arange(EXPERTS, dtype=jnp.int32), w_gate, w_up, w_down))
    return (rows_in.astype(jnp.float32) + routed).astype(jnp.bfloat16)


def reference(tokens, routes, route_weights, expert_gate, expert_up, expert_down):
    layer_out = lax.map(one_section, (tokens, routes.reshape(N_SECTION, TOKENS * TOPK), route_weights.reshape(N_SECTION, TOKENS * TOPK), expert_gate, expert_up, expert_down))
    next_input = jnp.concatenate([jnp.zeros_like(layer_out[:1]), layer_out[:-1]], axis=0)
    return layer_out, next_input
```

```python
import functools

import jax
import jax.numpy as jnp
from jax import lax
from jax.experimental import pallas as pl
from jax.experimental.pallas import tpu as pltpu
from jax.sharding import PartitionSpec as P

MESH = pl.DeviceIdType.MESH
CHIPS = 8
SENDS = 7
UP, DOWN = 0, 1


def kernel(
    tok_hbm, meta_hbm, gate_hbm, up_hbm, down_hbm,
    out_ref, next_ref,
    gath, meta, w_gate, w_up, w_down, contrib, rs_in, rs_out,
    local_sem, w_sem, w_send, w_recv,
    ag_send, ag_recv, meta_send, meta_recv, rs_send, rs_recv, hand_send, hand_recv,
):
    expert = lax.axis_index("expert")
    section = lax.axis_index("section")
    n_expert = 2 * CHIPS
    n_section = lax.axis_size("section")
    core = lax.rem(expert, 2)
    partner = expert + 1 - 2 * core
    neighbour = (
        {"expert": lax.rem(expert + 2, n_expert)},
        {"expert": lax.rem(expert + n_expert - 2, n_expert)},
    )
    after = {"section": lax.rem(section + 1, n_section)}
    before = {"section": lax.rem(section + n_section - 1, n_section)}
    half_rows = gath.shape[2]
    piece_rows = half_rows // 2

    own_tok = [
        pltpu.make_async_copy(
            tok_hbm.at[pl.ds(h * half_rows, half_rows)], gath.at[h, 0], local_sem.at[h]
        )
        for h in range(2)
    ]
    own_meta = pltpu.make_async_copy(meta_hbm, meta.at[0], local_sem.at[2])
    pairs = ((gate_hbm, w_gate), (up_hbm, w_up), (down_hbm, w_down))
    own_w = [
        pltpu.make_async_copy(src, dst.at[0], w_sem.at[i]) for i, (src, dst) in enumerate(pairs)
    ]
    for copy in own_tok + [own_meta] + own_w:
        copy.start()

    barrier = pltpu.get_barrier_semaphore()
    for device in (*neighbour, {"expert": partner}, after, before):
        pl.semaphore_signal(barrier, inc=1, device_id=device, device_id_type=MESH)
    pl.semaphore_wait(barrier, 5)

    def piece(ref, half, slot, part):
        return ref.at[half, slot, pl.ds(part * piece_rows, piece_rows)]

    def ag_copy(half, way, t):
        hop = t // 2
        if way == UP:
            part, source, target = t % 2, hop, hop + 1
        else:
            part, source, target = 1 - t % 2, (CHIPS - hop) % CHIPS, CHIPS - 1 - hop
        return pltpu.make_async_remote_copy(
            src_ref=piece(gath, half, source, part),
            dst_ref=piece(gath, half, target, part),
            send_sem=ag_send.at[half, way, t],
            recv_sem=ag_recv.at[half, target, part],
            device_id=neighbour[way],
            device_id_type=MESH,
        )

    def ag_wait(half, slot, part):
        ref = piece(gath, half, slot, part)
        pltpu.make_async_copy(ref, ref, ag_recv.at[half, slot, part]).wait()

    def ag_event(half, way, t):
        hop = t // 2
        if hop > 0:
            if way == UP:
                ag_wait(half, hop, t % 2)
            else:
                ag_wait(half, CHIPS - hop, 1 - t % 2)
        ag_copy(half, way, t).start()

    def meta_copy(way, hop):
        source, target = (hop, hop + 1) if way == UP else ((CHIPS - hop) % CHIPS, CHIPS - 1 - hop)
        return pltpu.make_async_remote_copy(
            src_ref=meta.at[source],
            dst_ref=meta.at[target],
            send_sem=meta_send.at[way, hop],
            recv_sem=meta_recv.at[target],
            device_id=neighbour[way],
            device_id_type=MESH,
        )

    def meta_wait(slot):
        pltpu.make_async_copy(meta.at[slot], meta.at[slot], meta_recv.at[slot]).wait()

    def meta_event(way, hop):
        if hop > 0:
            meta_wait(hop if way == UP else CHIPS - hop)
        meta_copy(way, hop).start()

    def w_copy(i):
        src, dst = pairs[i]
        return pltpu.make_async_remote_copy(
            src_ref=src,
            dst_ref=dst.at[1],
            send_sem=w_send.at[i],
            recv_sem=w_recv.at[i],
            device_id={"expert": partner},
            device_id_type=MESH,
        )

    own_tok[0].wait()
    own_meta.wait()
    for t in range(SENDS):
        for way in (UP, DOWN):
            ag_event(0, way, t)
            if way == UP and t % 2 == 0:
                meta_event(UP, t // 2)
            if way == DOWN and t % 2 == 1:
                meta_event(DOWN, t // 2)
        if t == 1:
            for i in range(3):
                w_copy(i).start()
            own_tok[1].wait()
    for copy in own_w:
        copy.wait()

    def rs_place(way, t):
        first = 1 if way == UP else 0
        if t == SENDS - 1:
            return 1 - first, 1, t - 1
        if t % 2 == 0:
            return first, 3 - t // 2, t - 2
        return 1 - first, 4 - t // 2, t - 2

    def rs_copy(half, way, t):
        return pltpu.make_async_remote_copy(
            src_ref=rs_out.at[half, way, t],
            dst_ref=rs_in.at[half, way, t],
            send_sem=rs_send.at[half, way, t],
            recv_sem=rs_recv.at[half, way, t],
            device_id=neighbour[way],
            device_id_type=MESH,
        )

    def rs_event(half, way, t):
        part, distance, previous = rs_place(way, t)
        slot = CHIPS - distance if way == UP else distance
        value = contrib[half, slot, pl.ds(part * piece_rows, piece_rows)]
        if previous >= 0:
            rs_copy(half, way, previous).wait_recv()
            value = value + rs_in[half, way, previous].astype(jnp.float32)
        rs_out[half, way, t] = value.astype(jnp.bfloat16)
        rs_copy(half, way, t).start()

    def column(slot, half, own):
        facts = meta[slot]
        weight = jnp.where(facts[0:1] == own, facts[2:3], 0.0) + jnp.where(
            facts[1:2] == own, facts[3:4], 0.0
        )
        shape = (half_rows, 2 * half_rows)
        row = lax.broadcasted_iota(jnp.int32, shape, 0) + half * half_rows
        lane = lax.broadcasted_iota(jnp.int32, shape, 1)
        spread = jnp.where(row == lane, jnp.broadcast_to(weight, shape), 0.0)
        return jnp.sum(spread, axis=1, keepdims=True)

    def compute(half, step):
        pair = lax.div(step, 2)
        which = lax.rem(step, 2)
        base = jnp.where(pair == 0, 0, jnp.where(pair == 1, 6, 2 * pair - 2))
        own = jnp.where(which == 0, expert, partner).astype(jnp.float32)
        rows = gath[half, pl.ds(base, 2)]
        rows = rows.reshape(2 * half_rows, rows.shape[2])
        gate_val = jnp.dot(rows, w_gate[which], preferred_element_type=jnp.float32)
        up_val = jnp.dot(rows, w_up[which], preferred_element_type=jnp.float32)
        hidden = (gate_val / (1.0 + jnp.exp(-gate_val)) * up_val).astype(jnp.bfloat16)
        result = jnp.dot(hidden, w_down[which], preferred_element_type=jnp.float32)

        for i in range(2):
            scaled = result[i * half_rows:(i + 1) * half_rows] * column(base + i, half, own)

            @pl.when(which == 0)
            def _():
                contrib[half, base + i] = scaled

            @pl.when(which == 1)
            def _():
                contrib[half, base + i] = contrib[half, base + i] + scaled

    @pl.loop(0, 16)
    def _(step):
        half = lax.div(step, 8)
        inner = lax.rem(step, 8)
        for t in range(SENDS):

            @pl.when(step == t)
            def _():
                for way in (UP, DOWN):
                    ag_event(1, way, t)

            @pl.when(step == 8 + t)
            def _():
                for way in (UP, DOWN):
                    rs_event(0, way, t)

        @pl.when(step == 1)
        def _():
            for i in range(3):
                w_copy(i).wait_recv()

        for h in range(2):

            @pl.when(step == 8 * h + 4)
            def _():
                ag_wait(h, 3, 1)

            @pl.when(step == 8 * h + 6)
            def _():
                ag_wait(h, 5, 0)
                ag_wait(h, 4, 0)
                ag_wait(h, 4, 1)

        @pl.when(step == 6)
        def _():
            meta_wait(4)
            meta_wait(5)

        compute(half, inner)

    def hand_copy(half):
        rows = pl.ds(half * half_rows, half_rows)
        return pltpu.make_async_remote_copy(
            src_ref=out_ref.at[rows],
            dst_ref=next_ref.at[rows],
            send_sem=hand_send.at[half],
            recv_sem=hand_recv.at[half],
            device_id=after,
            device_id_type=MESH,
        )

    def finish(half):
        for t in (4, 6):
            for way in (UP, DOWN):
                rs_copy(half, way, t).wait_recv()
        for part in range(2):
            rows = pl.ds(part * piece_rows, piece_rows)
            upward = rs_in[half, UP, 6 - 2 * part].astype(jnp.float32)
            downward = rs_in[half, DOWN, 4 + 2 * part].astype(jnp.float32)
            routed = contrib[half, 0, rows] + (upward + downward)
            total = gath[half, 0, rows].astype(jnp.float32) + routed
            out_ref[pl.ds(half * half_rows + part * piece_rows, piece_rows)] = total.astype(
                jnp.bfloat16
            )
        hand_copy(half).start()

    for t in range(SENDS):
        for way in (UP, DOWN):
            rs_event(1, way, t)
        if t == 1:
            finish(0)
    finish(1)

    for half in range(2):
        for way in (UP, DOWN):
            for t in range(SENDS):
                ag_copy(half, way, t).wait_send()
                rs_copy(half, way, t).wait_send()
    for way in (UP, DOWN):
        for hop in range(4 - way):
            meta_copy(way, hop).wait_send()
    for i in range(3):
        w_copy(i).wait_send()
    for half in range(2):
        hand_copy(half).wait()

    @pl.when(section == 0)
    def _():
        next_ref[...] = jnp.zeros_like(next_ref)


def per_device(tokens, routes, route_weights, expert_gate, expert_up, expert_down):
    rows_in = tokens[0]
    tok_count, width = rows_in.shape
    hidden = expert_gate.shape[3]
    facts = jnp.concatenate(
        [
            routes[0].astype(jnp.float32).T,
            route_weights[0].T,
            jnp.zeros((4, tok_count), jnp.float32),
        ]
    )
    half = tok_count // 2
    result = jax.ShapeDtypeStruct((tok_count, width), jnp.bfloat16)
    dma = pltpu.SemaphoreType.DMA
    layer_out, handed = pl.pallas_call(
        kernel,
        out_shape=(result, result),
        in_specs=[pl.BlockSpec(memory_space=pl.ANY)] * 5,
        out_specs=(pl.BlockSpec(memory_space=pltpu.VMEM),) * 2,
        scratch_shapes=[
            pltpu.VMEM((2, CHIPS, half, width), jnp.bfloat16),
            pltpu.VMEM((CHIPS, 8, tok_count), jnp.float32),
            pltpu.VMEM((2, width, hidden), jnp.bfloat16),
            pltpu.VMEM((2, width, hidden), jnp.bfloat16),
            pltpu.VMEM((2, hidden, width), jnp.bfloat16),
            pltpu.VMEM((2, CHIPS, half, width), jnp.float32),
            pltpu.VMEM((2, 2, SENDS, half // 2, width), jnp.bfloat16),
            pltpu.VMEM((2, 2, SENDS, half // 2, width), jnp.bfloat16),
            dma((3,)),
            dma((3,)),
            dma((3,)),
            dma((3,)),
            dma((2, 2, SENDS)),
            dma((2, CHIPS, 2)),
            dma((2, 4)),
            dma((CHIPS,)),
            dma((2, 2, SENDS)),
            dma((2, 2, SENDS)),
            dma((2,)),
            dma((2,)),
        ],
        compiler_params=pltpu.CompilerParams(
            collective_id=0, has_side_effects=True, vmem_limit_bytes=60 * 1024 * 1024
        ),
    )(rows_in, facts, expert_gate[0, 0], expert_up[0, 0], expert_down[0, 0])
    return (layer_out[None], handed[None])


def solution(mesh):
    in_specs = (
        P("section", ("expert", "tensor"), None),
        P("section", ("expert", "tensor"), None),
        P("section", ("expert", "tensor"), None),
        P("section", "expert", None, None),
        P("section", "expert", None, None),
        P("section", "expert", None, None),
    )
    out_specs = (P("section", ("expert", "tensor"), None), P("section", ("expert", "tensor"), None))
    return jax.shard_map(
        per_device, mesh=mesh, in_specs=in_specs, out_specs=out_specs, check_vma=False
    )
```

```python
import functools

import jax
import jax.numpy as jnp
from jax import lax
from jax.experimental import pallas as pl
from jax.experimental.pallas import tpu as pltpu
from jax.sharding import PartitionSpec as P

MESH = pl.DeviceIdType.MESH
CHIPS = 8
SENDS = 7
UP, DOWN = 0, 1
PARTS = 4


def kernel(
    tok_hbm, routes_ref, weights_ref, gate_hbm, up_hbm, down_hbm,
    out_ref, next_ref,
    gath, meta, w_gate, w_up, w_down, contrib, rs_in, rs_out,
    local_sem, w_sem, w_send, w_recv,
    ag_send, ag_recv, meta_send, meta_recv, rs_send, rs_recv, hand_send, hand_recv,
):
    expert = lax.axis_index("expert")
    section = lax.axis_index("section")
    n_expert = 2 * CHIPS
    n_section = lax.axis_size("section")
    core = lax.rem(expert, 2)
    partner = expert + 1 - 2 * core
    neighbour = (
        {"expert": lax.rem(expert + 2, n_expert)},
        {"expert": lax.rem(expert + n_expert - 2, n_expert)},
    )
    after = {"section": lax.rem(section + 1, n_section)}
    before = {"section": lax.rem(section + n_section - 1, n_section)}
    half_rows = gath.shape[2]
    piece_rows = half_rows // 2

    own_tok = [
        pltpu.make_async_copy(
            tok_hbm.at[pl.ds(h * half_rows, half_rows)], gath.at[h, 0], local_sem.at[h]
        )
        for h in range(2)
    ]
    pairs = ((gate_hbm, w_gate), (up_hbm, w_up), (down_hbm, w_down))
    own_w = [
        pltpu.make_async_copy(src, dst.at[0], w_sem.at[i]) for i, (src, dst) in enumerate(pairs)
    ]
    for copy in own_tok + own_w:
        copy.start()
    meta[0, 0:2] = routes_ref[...].astype(jnp.float32)
    meta[0, 2:4] = weights_ref[...]
    meta[0, 4:8] = jnp.zeros((4, meta.shape[2]), jnp.float32)

    barrier = pltpu.get_barrier_semaphore()
    for device in (*neighbour, {"expert": partner}, after, before):
        pl.semaphore_signal(barrier, inc=1, device_id=device, device_id_type=MESH)
    pl.semaphore_wait(barrier, 5)

    def piece(ref, half, slot, part):
        return ref.at[half, slot, pl.ds(part * piece_rows, piece_rows)]

    def ag_copy(half, way, t):
        hop = t // 2
        if way == UP:
            part, source, target = t % 2, hop, hop + 1
        else:
            part, source, target = 1 - t % 2, (CHIPS - hop) % CHIPS, CHIPS - 1 - hop
        return pltpu.make_async_remote_copy(
            src_ref=piece(gath, half, source, part),
            dst_ref=piece(gath, half, target, part),
            send_sem=ag_send.at[half, way, t],
            recv_sem=ag_recv.at[half, target, part],
            device_id=neighbour[way],
            device_id_type=MESH,
        )

    def ag_wait(half, slot, part):
        ref = piece(gath, half, slot, part)
        pltpu.make_async_copy(ref, ref, ag_recv.at[half, slot, part]).wait()

    def ag_event(half, way, t):
        hop = t // 2
        if hop > 0:
            if way == UP:
                ag_wait(half, hop, t % 2)
            else:
                ag_wait(half, CHIPS - hop, 1 - t % 2)
        ag_copy(half, way, t).start()

    def meta_copy(way, hop):
        source, target = (hop, hop + 1) if way == UP else ((CHIPS - hop) % CHIPS, CHIPS - 1 - hop)
        return pltpu.make_async_remote_copy(
            src_ref=meta.at[source],
            dst_ref=meta.at[target],
            send_sem=meta_send.at[way, hop],
            recv_sem=meta_recv.at[target],
            device_id=neighbour[way],
            device_id_type=MESH,
        )

    def meta_wait(slot):
        pltpu.make_async_copy(meta.at[slot], meta.at[slot], meta_recv.at[slot]).wait()

    def meta_event(way, hop):
        if hop > 0:
            meta_wait(hop if way == UP else CHIPS - hop)
        meta_copy(way, hop).start()

    def w_copy(i):
        src, dst = pairs[i]
        return pltpu.make_async_remote_copy(
            src_ref=src,
            dst_ref=dst.at[1],
            send_sem=w_send.at[i],
            recv_sem=w_recv.at[i],
            device_id={"expert": partner},
            device_id_type=MESH,
        )

    own_tok[0].wait()
    for t in range(SENDS):
        for way in (UP, DOWN):
            ag_event(0, way, t)
            if way == UP and t % 2 == 0:
                meta_event(UP, t // 2)
            if way == DOWN and t % 2 == 1:
                meta_event(DOWN, t // 2)
        if t == 1:
            for i in range(3):
                w_copy(i).start()
            own_tok[1].wait()
    for copy in own_w:
        copy.wait()

    def rs_place(way, t):
        first = 1 if way == UP else 0
        if t == SENDS - 1:
            return 1 - first, 1, t - 1
        if t % 2 == 0:
            return first, 3 - t // 2, t - 2
        return 1 - first, 4 - t // 2, t - 2

    def rs_copy(half, way, t):
        return pltpu.make_async_remote_copy(
            src_ref=rs_out.at[half, way, t],
            dst_ref=rs_in.at[half, way, t],
            send_sem=rs_send.at[half, way, t],
            recv_sem=rs_recv.at[half, way, t],
            device_id=neighbour[way],
            device_id_type=MESH,
        )

    def rs_event(half, way, t):
        part, distance, previous = rs_place(way, t)
        slot = CHIPS - distance if way == UP else distance
        value = contrib[half, slot, pl.ds(part * piece_rows, piece_rows)]
        if previous >= 0:
            rs_copy(half, way, previous).wait_recv()
            value = value + rs_in[half, way, previous].astype(jnp.float32)
        rs_out[half, way, t] = value.astype(jnp.bfloat16)
        rs_copy(half, way, t).start()

    def column(slot, half, own):
        facts = meta[slot]
        weight = jnp.where(facts[0:1] == own, facts[2:3], 0.0) + jnp.where(
            facts[1:2] == own, facts[3:4], 0.0
        )
        shape = (half_rows, 2 * half_rows)
        row = lax.broadcasted_iota(jnp.int32, shape, 0) + half * half_rows
        lane = lax.broadcasted_iota(jnp.int32, shape, 1)
        spread = jnp.where(row == lane, jnp.broadcast_to(weight, shape), 0.0)
        return jnp.sum(spread, axis=1, keepdims=True)

    def compute(half, step):
        pair = lax.div(step, 2)
        which = lax.rem(step, 2)
        base = jnp.where(pair == 0, 6, jnp.where(pair == 3, 0, 2 * pair))
        own = jnp.where(which == 0, expert, partner).astype(jnp.float32)
        rows = gath[half, pl.ds(base, 2)]
        rows = rows.reshape(2 * half_rows, rows.shape[2])
        gate_val = jnp.dot(rows, w_gate[which], preferred_element_type=jnp.float32)
        up_val = jnp.dot(rows, w_up[which], preferred_element_type=jnp.float32)
        hidden = (gate_val / (1.0 + jnp.exp(-gate_val)) * up_val).astype(jnp.bfloat16)
        result = jnp.dot(hidden, w_down[which], preferred_element_type=jnp.float32)

        for i in range(2):
            scaled = result[i * half_rows:(i + 1) * half_rows] * column(base + i, half, own)

            @pl.when(which == 0)
            def _():
                contrib[half, base + i] = scaled

            @pl.when(which == 1)
            def _():
                contrib[half, base + i] = contrib[half, base + i] + scaled

    @pl.loop(0, 16)
    def _(step):
        half = lax.div(step, 8)
        inner = lax.rem(step, 8)
        for t in range(SENDS):

            @pl.when(step == t)
            def _():
                for way in (UP, DOWN):
                    ag_event(1, way, t)

            @pl.when(step == 7 + t)
            def _():
                for way in (UP, DOWN):
                    rs_event(0, way, t)

        for t in range(2):

            @pl.when(step == 14 + t)
            def _():
                for way in (UP, DOWN):
                    rs_event(1, way, t)

        @pl.when(step == 1)
        def _():
            for i in range(3):
                w_copy(i).wait_recv()

        for h in range(2):

            @pl.when(step == 8 * h + 2)
            def _():
                ag_wait(h, 3, 1)

            @pl.when(step == 8 * h + 4)
            def _():
                ag_wait(h, 5, 0)
                ag_wait(h, 4, 0)
                ag_wait(h, 4, 1)

        @pl.when(step == 4)
        def _():
            meta_wait(4)
            meta_wait(5)

        compute(half, inner)

    def hand_copy(half):
        rows = pl.ds(half * half_rows, half_rows)
        return pltpu.make_async_remote_copy(
            src_ref=out_ref.at[rows],
            dst_ref=next_ref.at[rows],
            send_sem=hand_send.at[half],
            recv_sem=hand_recv.at[half],
            device_id=after,
            device_id_type=MESH,
        )

    def finish(half):
        for t in (4, 6):
            for way in (UP, DOWN):
                rs_copy(half, way, t).wait_recv()
        for part in range(2):
            rows = pl.ds(part * piece_rows, piece_rows)
            upward = rs_in[half, UP, 6 - 2 * part].astype(jnp.float32)
            downward = rs_in[half, DOWN, 4 + 2 * part].astype(jnp.float32)
            routed = contrib[half, 0, rows] + (upward + downward)
            total = gath[half, 0, rows].astype(jnp.float32) + routed
            out_ref[pl.ds(half * half_rows + part * piece_rows, piece_rows)] = total.astype(
                jnp.bfloat16
            )
        hand_copy(half).start()

    finish(0)
    for t in range(2, SENDS):
        for way in (UP, DOWN):
            rs_event(1, way, t)
    finish(1)

    for half in range(2):
        for way in (UP, DOWN):
            for t in range(SENDS):
                ag_copy(half, way, t).wait_send()
                rs_copy(half, way, t).wait_send()
    for way in (UP, DOWN):
        for hop in range(4 - way):
            meta_copy(way, hop).wait_send()
    for i in range(3):
        w_copy(i).wait_send()
    for half in range(2):
        hand_copy(half).wait()

    @pl.when(section == 0)
    def _():
        next_ref[...] = jnp.zeros_like(next_ref)


def place(layer_ref, hand_ref, layer_out, hand_out, held, in_sem, out_sem):
    ends = ((layer_ref, layer_out), (hand_ref, hand_out))
    rows = layer_ref.shape[0] // PARTS
    inward, outward = [], []
    for part in range(PARTS):
        where = pl.ds(part * rows, rows)
        for i, (source, target) in enumerate(ends):
            block = held.at[i, where]
            inward.append(pltpu.make_async_copy(source.at[where], block, in_sem.at[i, part]))
            outward.append(pltpu.make_async_copy(block, target.at[where], out_sem.at[i, part]))
    for copy in inward:
        copy.start()
    for arrival, departure in zip(inward, outward):
        arrival.wait()
        departure.start()
    for copy in outward:
        copy.wait()


def per_device(tokens, routes, route_weights, expert_gate, expert_up, expert_down):
    rows_in = tokens[0]
    tok_count, width = rows_in.shape
    hidden = expert_gate.shape[3]
    half = tok_count // 2
    result = jax.ShapeDtypeStruct((tok_count, width), jnp.bfloat16)
    dma = pltpu.SemaphoreType.DMA
    layer_out, handed = pl.pallas_call(
        kernel,
        out_shape=(result, result),
        in_specs=[pl.BlockSpec(memory_space=pl.ANY)]
        + [pl.BlockSpec(memory_space=pltpu.VMEM)] * 2
        + [pl.BlockSpec(memory_space=pl.ANY)] * 3,
        out_specs=(pl.BlockSpec(memory_space=pltpu.VMEM),) * 2,
        scratch_shapes=[
            pltpu.VMEM((2, CHIPS, half, width), jnp.bfloat16),
            pltpu.VMEM((CHIPS, 8, tok_count), jnp.float32),
            pltpu.VMEM((2, width, hidden), jnp.bfloat16),
            pltpu.VMEM((2, width, hidden), jnp.bfloat16),
            pltpu.VMEM((2, hidden, width), jnp.bfloat16),
            pltpu.VMEM((2, CHIPS, half, width), jnp.float32),
            pltpu.VMEM((2, 2, SENDS, half // 2, width), jnp.bfloat16),
            pltpu.VMEM((2, 2, SENDS, half // 2, width), jnp.bfloat16),
            dma((2,)),
            dma((3,)),
            dma((3,)),
            dma((3,)),
            dma((2, 2, SENDS)),
            dma((2, CHIPS, 2)),
            dma((2, 4)),
            dma((CHIPS,)),
            dma((2, 2, SENDS)),
            dma((2, 2, SENDS)),
            dma((2,)),
            dma((2,)),
        ],
        compiler_params=pltpu.CompilerParams(
            collective_id=0, has_side_effects=True, vmem_limit_bytes=60 * 1024 * 1024
        ),
    )(
        rows_in,
        routes[0].T,
        route_weights[0].T,
        expert_gate[0, 0],
        expert_up[0, 0],
        expert_down[0, 0],
    )
    layer_out, handed = pl.pallas_call(
        place,
        out_shape=(result, result),
        in_specs=[pl.BlockSpec(memory_space=pl.ANY)] * 2,
        out_specs=(pl.BlockSpec(memory_space=pl.ANY),) * 2,
        scratch_shapes=[
            pltpu.VMEM((2, tok_count, width), jnp.bfloat16),
            dma((2, PARTS)),
            dma((2, PARTS)),
        ],
    )(layer_out, handed)
    return (layer_out[None], handed[None])


def solution(mesh):
    in_specs = (
        P("section", ("expert", "tensor"), None),
        P("section", ("expert", "tensor"), None),
        P("section", ("expert", "tensor"), None),
        P("section", "expert", None, None),
        P("section", "expert", None, None),
        P("section", "expert", None, None),
    )
    out_specs = (P("section", ("expert", "tensor"), None), P("section", ("expert", "tensor"), None))
    return jax.shard_map(
        per_device, mesh=mesh, in_specs=in_specs, out_specs=out_specs, check_vma=False
    )
```

```python
import functools

import jax
import jax.numpy as jnp
from jax import lax
from jax.experimental import pallas as pl
from jax.experimental.pallas import tpu as pltpu
from jax.sharding import PartitionSpec as P

MESH = pl.DeviceIdType.MESH
CHIPS = 8
SENDS = 7
UP, DOWN = 0, 1
PARTS = 4
LAG = 5


def kernel(
    tok_hbm, routes_ref, weights_ref, gate_hbm, up_hbm, down_hbm,
    out_ref, next_ref,
    gath, meta, w_gate, w_up, w_down, contrib, rs_in, rs_out,
    local_sem, w_sem, w_send, w_recv,
    ag_send, ag_recv, meta_send, meta_recv, rs_send, rs_recv, hand_send, hand_recv,
):
    expert = lax.axis_index("expert")
    section = lax.axis_index("section")
    n_expert = 2 * CHIPS
    n_section = lax.axis_size("section")
    core = lax.rem(expert, 2)
    partner = expert + 1 - 2 * core
    neighbour = (
        {"expert": lax.rem(expert + 2, n_expert)},
        {"expert": lax.rem(expert + n_expert - 2, n_expert)},
    )
    after = {"section": lax.rem(section + 1, n_section)}
    before = {"section": lax.rem(section + n_section - 1, n_section)}
    half_rows = gath.shape[2]
    piece_rows = half_rows // 2

    own_tok = [
        pltpu.make_async_copy(
            tok_hbm.at[pl.ds(h * half_rows, half_rows)], gath.at[h, 0], local_sem.at[h]
        )
        for h in range(2)
    ]
    pairs = ((gate_hbm, w_gate), (up_hbm, w_up), (down_hbm, w_down))
    own_w = [
        pltpu.make_async_copy(src, dst.at[0], w_sem.at[i]) for i, (src, dst) in enumerate(pairs)
    ]
    for copy in own_tok + own_w:
        copy.start()
    meta[0, 0:2] = routes_ref[...].astype(jnp.float32)
    meta[0, 2:4] = weights_ref[...]
    meta[0, 4:8] = jnp.zeros((4, meta.shape[2]), jnp.float32)

    barrier = pltpu.get_barrier_semaphore()
    for device in (*neighbour, {"expert": partner}, after, before):
        pl.semaphore_signal(barrier, inc=1, device_id=device, device_id_type=MESH)
    pl.semaphore_wait(barrier, 5)

    def piece(ref, half, slot, part):
        return ref.at[half, slot, pl.ds(part * piece_rows, piece_rows)]

    def ag_copy(half, way, t):
        hop = t // 2
        if way == UP:
            part, source, target = t % 2, hop, hop + 1
        else:
            part, source, target = 1 - t % 2, (CHIPS - hop) % CHIPS, CHIPS - 1 - hop
        return pltpu.make_async_remote_copy(
            src_ref=piece(gath, half, source, part),
            dst_ref=piece(gath, half, target, part),
            send_sem=ag_send.at[half, way, t],
            recv_sem=ag_recv.at[half, target, part],
            device_id=neighbour[way],
            device_id_type=MESH,
        )

    def ag_wait(half, slot, part):
        ref = piece(gath, half, slot, part)
        pltpu.make_async_copy(ref, ref, ag_recv.at[half, slot, part]).wait()

    def ag_event(half, way, t):
        hop = t // 2
        if hop > 0:
            if way == UP:
                ag_wait(half, hop, t % 2)
            else:
                ag_wait(half, CHIPS - hop, 1 - t % 2)
        ag_copy(half, way, t).start()

    def meta_copy(way, hop):
        source, target = (hop, hop + 1) if way == UP else ((CHIPS - hop) % CHIPS, CHIPS - 1 - hop)
        return pltpu.make_async_remote_copy(
            src_ref=meta.at[source],
            dst_ref=meta.at[target],
            send_sem=meta_send.at[way, hop],
            recv_sem=meta_recv.at[target],
            device_id=neighbour[way],
            device_id_type=MESH,
        )

    def meta_wait(slot):
        pltpu.make_async_copy(meta.at[slot], meta.at[slot], meta_recv.at[slot]).wait()

    def meta_event(way, hop):
        if hop > 0:
            meta_wait(hop if way == UP else CHIPS - hop)
        meta_copy(way, hop).start()

    def w_copy(i):
        src, dst = pairs[i]
        return pltpu.make_async_remote_copy(
            src_ref=src,
            dst_ref=dst.at[1],
            send_sem=w_send.at[i],
            recv_sem=w_recv.at[i],
            device_id={"expert": partner},
            device_id_type=MESH,
        )

    own_tok[0].wait()
    for t in range(SENDS):
        for way in (UP, DOWN):
            ag_event(0, way, t)
            if way == UP and t % 2 == 0:
                meta_event(UP, t // 2)
            if way == DOWN and t % 2 == 1:
                meta_event(DOWN, t // 2)
        if t == 1:
            for i in range(3):
                w_copy(i).start()
            own_tok[1].wait()
    for copy in own_w:
        copy.wait()

    def rs_place(way, t):
        first = 1 if way == UP else 0
        if t == SENDS - 1:
            return 1 - first, 1, t - 1
        if t % 2 == 0:
            return first, 3 - t // 2, t - 2
        return 1 - first, 4 - t // 2, t - 2

    def rs_rows(half, sub):
        count = piece_rows // (1 + half)
        return sub * count, count

    def rs_copy(half, way, t, sub=0):
        rows = pl.ds(*rs_rows(half, sub))
        return pltpu.make_async_remote_copy(
            src_ref=rs_out.at[half, way, t, rows],
            dst_ref=rs_in.at[half, way, t, rows],
            send_sem=rs_send.at[half + sub, way, t],
            recv_sem=rs_recv.at[half + sub, way, t],
            device_id=neighbour[way],
            device_id_type=MESH,
        )

    def rs_event(half, way, t, sub=0):
        part, distance, previous = rs_place(way, t)
        slot = CHIPS - distance if way == UP else distance
        start, count = rs_rows(half, sub)
        rows = pl.ds(start, count)
        value = contrib[half, slot, pl.ds(part * piece_rows + start, count)]
        if previous >= 0:
            rs_copy(half, way, previous, sub).wait_recv()
            value = value + rs_in[half, way, previous, rows].astype(jnp.float32)
        rs_out[half, way, t, rows] = value.astype(jnp.bfloat16)
        rs_copy(half, way, t, sub).start()

    def column(slot, half, own):
        facts = meta[slot]
        weight = jnp.where(facts[0:1] == own, facts[2:3], 0.0) + jnp.where(
            facts[1:2] == own, facts[3:4], 0.0
        )
        shape = (half_rows, 2 * half_rows)
        row = lax.broadcasted_iota(jnp.int32, shape, 0) + half * half_rows
        lane = lax.broadcasted_iota(jnp.int32, shape, 1)
        spread = jnp.where(row == lane, jnp.broadcast_to(weight, shape), 0.0)
        return jnp.sum(spread, axis=1, keepdims=True)

    def compute(half, step):
        pair = lax.div(step, 2)
        which = lax.rem(step, 2)
        base = jnp.where(pair == 0, 6, jnp.where(pair == 3, 0, 2 * pair))
        own = jnp.where(which == 0, expert, partner).astype(jnp.float32)
        rows = gath[half, pl.ds(base, 2)]
        rows = rows.reshape(2 * half_rows, rows.shape[2])
        gate_val = jnp.dot(rows, w_gate[which], preferred_element_type=jnp.float32)
        up_val = jnp.dot(rows, w_up[which], preferred_element_type=jnp.float32)
        hidden = (gate_val / (1.0 + jnp.exp(-gate_val)) * up_val).astype(jnp.bfloat16)
        result = jnp.dot(hidden, w_down[which], preferred_element_type=jnp.float32)

        for i in range(2):
            scaled = result[i * half_rows:(i + 1) * half_rows] * column(base + i, half, own)

            @pl.when(which == 0)
            def _():
                contrib[half, base + i] = scaled

            @pl.when(which == 1)
            def _():
                contrib[half, base + i] = contrib[half, base + i] + scaled

    @pl.loop(0, 16)
    def _(step):
        half = lax.div(step, 8)
        inner = lax.rem(step, 8)
        for t in range(SENDS):

            @pl.when(step == t)
            def _():
                for way in (UP, DOWN):
                    ag_event(1, way, t)

            @pl.when(step == 7 + t)
            def _():
                for way in (UP, DOWN):
                    rs_event(0, way, t)

        for t in range(2):

            @pl.when(step == 14 + t)
            def _():
                for way in (UP, DOWN):
                    rs_event(1, way, t)

        @pl.when(step == 1)
        def _():
            for i in range(3):
                w_copy(i).wait_recv()

        for h in range(2):

            @pl.when(step == 8 * h + 2)
            def _():
                ag_wait(h, 3, 1)

            @pl.when(step == 8 * h + 4)
            def _():
                ag_wait(h, 5, 0)
                ag_wait(h, 4, 0)
                ag_wait(h, 4, 1)

        @pl.when(step == 4)
        def _():
            meta_wait(4)
            meta_wait(5)

        compute(half, inner)

    def hand_copy(half, part, sub=0):
        start, count = rs_rows(half, sub)
        rows = pl.ds(half * half_rows + part * piece_rows + start, count)
        return pltpu.make_async_remote_copy(
            src_ref=out_ref.at[rows],
            dst_ref=next_ref.at[rows],
            send_sem=hand_send.at[half + sub, part],
            recv_sem=hand_recv.at[half + sub, part],
            device_id=after,
            device_id_type=MESH,
        )

    def finish(half, sub=0):
        for t in (4, 6):
            for way in (UP, DOWN):
                rs_copy(half, way, t, sub).wait_recv()
        start, count = rs_rows(half, sub)
        for part in range(2):
            rows = pl.ds(part * piece_rows + start, count)
            upward = rs_in[half, UP, 6 - 2 * part, pl.ds(start, count)].astype(jnp.float32)
            downward = rs_in[half, DOWN, 4 + 2 * part, pl.ds(start, count)].astype(jnp.float32)
            routed = contrib[half, 0, rows] + (upward + downward)
            total = gath[half, 0, rows].astype(jnp.float32) + routed
            out_ref[pl.ds(half * half_rows + part * piece_rows + start, count)] = total.astype(
                jnp.bfloat16
            )
            hand_copy(half, part, sub).start()

    finish(0)
    for t in range(2, SENDS + LAG):
        for way in (UP, DOWN):
            if t < SENDS:
                rs_event(1, way, t, 0)
            if t >= LAG:
                rs_event(1, way, t - LAG, 1)
        if t == SENDS:
            finish(1, 0)
    finish(1, 1)

    for half in range(2):
        for way in (UP, DOWN):
            for t in range(SENDS):
                ag_copy(half, way, t).wait_send()
                for sub in range(1 + half):
                    rs_copy(half, way, t, sub).wait_send()
    for way in (UP, DOWN):
        for hop in range(4 - way):
            meta_copy(way, hop).wait_send()
    for i in range(3):
        w_copy(i).wait_send()
    for half in range(2):
        for sub in range(1 + half):
            for part in range(2):
                hand_copy(half, part, sub).wait()

    @pl.when(section == 0)
    def _():
        next_ref[...] = jnp.zeros_like(next_ref)


def place(layer_ref, hand_ref, layer_out, hand_out, held, in_sem, out_sem):
    ends = ((layer_ref, layer_out), (hand_ref, hand_out))
    rows = layer_ref.shape[0] // PARTS
    inward, outward = [], []
    for part in range(PARTS):
        where = pl.ds(part * rows, rows)
        for i, (source, target) in enumerate(ends):
            block = held.at[i, where]
            inward.append(pltpu.make_async_copy(source.at[where], block, in_sem.at[i, part]))
            outward.append(pltpu.make_async_copy(block, target.at[where], out_sem.at[i, part]))
    for copy in inward:
        copy.start()
    for arrival, departure in zip(inward, outward):
        arrival.wait()
        departure.start()
    for copy in outward:
        copy.wait()


def per_device(tokens, routes, route_weights, expert_gate, expert_up, expert_down):
    rows_in = tokens[0]
    tok_count, width = rows_in.shape
    hidden = expert_gate.shape[3]
    half = tok_count // 2
    result = jax.ShapeDtypeStruct((tok_count, width), jnp.bfloat16)
    dma = pltpu.SemaphoreType.DMA
    layer_out, handed = pl.pallas_call(
        kernel,
        out_shape=(result, result),
        in_specs=[pl.BlockSpec(memory_space=pl.ANY)]
        + [pl.BlockSpec(memory_space=pltpu.VMEM)] * 2
        + [pl.BlockSpec(memory_space=pl.ANY)] * 3,
        out_specs=(pl.BlockSpec(memory_space=pltpu.VMEM),) * 2,
        scratch_shapes=[
            pltpu.VMEM((2, CHIPS, half, width), jnp.bfloat16),
            pltpu.VMEM((CHIPS, 8, tok_count), jnp.float32),
            pltpu.VMEM((2, width, hidden), jnp.bfloat16),
            pltpu.VMEM((2, width, hidden), jnp.bfloat16),
            pltpu.VMEM((2, hidden, width), jnp.bfloat16),
            pltpu.VMEM((2, CHIPS, half, width), jnp.float32),
            pltpu.VMEM((2, 2, SENDS, half // 2, width), jnp.bfloat16),
            pltpu.VMEM((2, 2, SENDS, half // 2, width), jnp.bfloat16),
            dma((2,)),
            dma((3,)),
            dma((3,)),
            dma((3,)),
            dma((2, 2, SENDS)),
            dma((2, CHIPS, 2)),
            dma((2, 4)),
            dma((CHIPS,)),
            dma((3, 2, SENDS)),
            dma((3, 2, SENDS)),
            dma((3, 2)),
            dma((3, 2)),
        ],
        compiler_params=pltpu.CompilerParams(
            collective_id=0, has_side_effects=True, vmem_limit_bytes=60 * 1024 * 1024
        ),
    )(
        rows_in,
        routes[0].T,
        route_weights[0].T,
        expert_gate[0, 0],
        expert_up[0, 0],
        expert_down[0, 0],
    )
    layer_out, handed = pl.pallas_call(
        place,
        out_shape=(result, result),
        in_specs=[pl.BlockSpec(memory_space=pl.ANY)] * 2,
        out_specs=(pl.BlockSpec(memory_space=pl.ANY),) * 2,
        scratch_shapes=[
            pltpu.VMEM((2, tok_count, width), jnp.bfloat16),
            dma((2, PARTS)),
            dma((2, PARTS)),
        ],
    )(layer_out, handed)
    return (layer_out[None], handed[None])


def solution(mesh):
    in_specs = (
        P("section", ("expert", "tensor"), None),
        P("section", ("expert", "tensor"), None),
        P("section", ("expert", "tensor"), None),
        P("section", "expert", None, None),
        P("section", "expert", None, None),
        P("section", "expert", None, None),
    )
    out_specs = (P("section", ("expert", "tensor"), None), P("section", ("expert", "tensor"), None))
    return jax.shard_map(
        per_device, mesh=mesh, in_specs=in_specs, out_specs=out_specs, check_vma=False
    )
```
